32 devices in a mesh: dp: 8 (over y, x, core), tensor: 4 (over z).
Axes of the slice: x: 2, y: 2, z: 4, core: 2. Of those that a mesh axis runs over, the one named last changes fastest.
Arguments:
- block_in: float32 [4096, 1024], P(('dp', 'tensor')), may hold values from -6 to 6
- cotangent: float32 [4096, 1024], P(('dp', 'tensor')), may hold values from -6 to 6
- routes: int32 [4096, 8], P('dp'), may hold values from 0 to 15, all different within a row; in each aligned block of 512 rows (0 to 511, 512 to 1023, ...) at most 288 rows name the same one
- gate_weights: float32 [4096, 8], P('dp'), may hold values from 0.02 to 0.3
- norm_gains: float32 [2, 1024], P(None, 'dp'), may hold values from 0.5 to 1.5
- attention_weight: float32 [4, 1024, 512], P(None, 'dp', 'tensor'), may hold values from -0.1875 to 0.1875
- output_weight: float32 [2, 1024, 512], P(None, 'dp', 'tensor'), may hold values from -0.75 to 0.75
- w_gate_up: float32 [16, 2, 1024, 512], P(None, None, 'dp', 'tensor'), may hold values from -0.1875 to 0.1875
- w_down: float32 [16, 1024, 512], P(None, 'dp', 'tensor'), may hold values from -0.75 to 0.75
- m_gains: float32 [2, 1024], P(None, 'dp'), may hold values from -128 to 128
- v_gains: float32 [2, 1024], P(None, 'dp'), may hold values from 100 to 10000
- attention_first_moment: float32 [4, 1024, 512], P(None, 'dp', 'tensor'), may hold values from -12 to 12
- attention_second_moment: float32 [4, 1024, 512], P(None, 'dp', 'tensor'), may hold values from 1 to 100
- output_first_moment: float32 [2, 1024, 512], P(None, 'dp', 'tensor'), may hold values from -16 to 16
- output_second_moment: float32 [2, 1024, 512], P(None, 'dp', 'tensor'), may hold values from 1 to 100
- m_gate_up: float32 [16, 2, 1024, 512], P(None, None, 'dp', 'tensor'), may hold values from -32 to 32
- v_gate_up: float32 [16, 2, 1024, 512], P(None, None, 'dp', 'tensor'), may hold values from 10 to 1000
- m_down: float32 [16, 1024, 512], P(None, 'dp', 'tensor'), may hold values from -12 to 12
- v_down: float32 [16, 1024, 512], P(None, 'dp', 'tensor'), may hold values from 1 to 100
Outputs:
- block_out: float32 [4096, 1024], P(('dp', 'tensor'))
- input_grad: float32 [4096, 1024], P(('dp', 'tensor'))
- grad_gains: float32 [2, 1024], P(None, 'dp')
- grad_attn: float32 [4, 1024, 512], P(None, 'dp', 'tensor')
- grad_out: float32 [2, 1024, 512], P(None, 'dp', 'tensor')
- grad_gate_up: float32 [16, 2, 1024, 512], P(None, None, 'dp', 'tensor')
- grad_down: float32 [16, 1024, 512], P(None, 'dp', 'tensor')
- new_gains: float32 [2, 1024], P(None, 'dp')
- new_attn: float32 [4, 1024, 512], P(None, 'dp', 'tensor')
- new_out: float32 [2, 1024, 512], P(None, 'dp', 'tensor')
- new_gate_up: float32 [16, 2, 1024, 512], P(None, None, 'dp', 'tensor')
- new_down: float32 [16, 1024, 512], P(None, 'dp', 'tensor')
- new_m_gains: float32 [2, 1024], P(None, 'dp')
- new_v_gains: float32 [2, 1024], P(None, 'dp')
- new_m_attn: float32 [4, 1024, 512], P(None, 'dp', 'tensor')
- new_v_attn: float32 [4, 1024, 512], P(None, 'dp', 'tensor')
- new_m_out: float32 [2, 1024, 512], P(None, 'dp', 'tensor')
- new_v_out: float32 [2, 1024, 512], P(None, 'dp', 'tensor')
- new_m_gate_up: float32 [16, 2, 1024, 512], P(None, None, 'dp', 'tensor')
- new_v_gate_up: float32 [16, 2, 1024, 512], P(None, None, 'dp', 'tensor')
- new_m_down: float32 [16, 1024, 512], P(None, 'dp', 'tensor')
- new_v_down: float32 [16, 1024, 512], P(None, 'dp', 'tensor')
The draws below stay inside these ranges and needn't reach their ends.
Inputs may be any that keep to these rules, and one draw needn't show every extreme that they name: `routes`: each row names 8 different experts. Within each aligned block of 512 rows no expert is named by more than 288 rows, and in some block one expert is named by exactly 288 rows.
All inputs are finite; a program needn't handle non-finite values.
Results may differ from the reference program's by a relative error of at most 0.015.
The reference program's roundings to bfloat16 on the way count: a program that leaves them out, or rounds other values in their place, can miss the bound.
Values may be sent and summed in bfloat16 or wider, within the bound.
A program may use at most 192 MiB of HBM per device.

```python
import math
import jax
import jax.numpy as jnp
import numpy as np
from jax import lax

MODEL_WIDTH = 1024
QUERY_HEADS = 16
KEY_VALUE_HEADS = 8
HEAD_SIZE = 64
E = 16
FF = 512
TOPK = 8
SEQ = 512
SEQS = 1
STEP = 3
TOKENS = 4096
CAP = 288
N_DP = 8


def block_levels(own_key, shape, split, smallest, top_value):
    level, own = 1.0, jax.random.fold_in(own_key, 6)
    for axis_at, shards_of in split:
        heights = jnp.exp(jax.random.uniform(jax.random.fold_in(own, axis_at), (shards_of,), jnp.float32, smallest / len(split), top_value / len(split)))
        level = level * jnp.repeat(heights, shape[axis_at] // shards_of).reshape([-1 if axis == axis_at else 1 for axis in range(len(shape))])
    return level


def deal_out(own_key, own, number, rows, number_of, top, reach, slope):
    sequence = jax.random.permutation(own_key, number_of)
    heavy_load, usual = portions_of(number_of, rows * top, reach, slope, True), portions_of(number_of, rows * top, reach, slope, False)
    places = jnp.arange(number_of)

    def named(tallies, offset_by):
        used = int((tallies > 0).sum())
        fixed = max(1, used // 4)
        passed = fixed + (places - fixed + offset_by * (used - fixed)) % max(1, number_of - fixed)
        return jnp.zeros((number_of,), jnp.int32).at[sequence[jnp.where(places < fixed, places, passed)]].set(jnp.asarray(tallies, jnp.int32))

    tallies = jnp.where(number % 4 == 0, named(heavy_load, number // 4), named(usual, number - number // 4 - 1))
    mixed = jax.random.permutation(jax.random.fold_in(own, 3), number_of)
    donor, receiver = mixed[0:number_of // 2 * 2:2], mixed[1:number_of // 2 * 2:2]
    slack = jnp.minimum(tallies[donor] - 1, reach - tallies[receiver]) // 2
    slack = jnp.where((donor == sequence[0]) | (receiver == sequence[0]) | (tallies[receiver] == 0), 0, jnp.maximum(slack, 0))
    passed = jax.random.randint(jax.random.fold_in(own, 4), (number_of // 2,), 0, 1 << 20) % (slack + 1)
    tallies = tallies.at[donor].add(-passed).at[receiver].add(passed)
    items = jnp.searchsorted(jnp.cumsum(tallies), jnp.arange(rows * top), side="right").astype(jnp.int32)
    listing = items.reshape(top, rows).T
    listing = listing[jax.random.permutation(jax.random.fold_in(own, 1), rows)]
    offset_by = jax.random.randint(jax.random.fold_in(own, 2), (rows, 1), 0, top)
    return jnp.take_along_axis(listing, (jnp.arange(top)[None, :] + offset_by) % top, axis=1)


def portions_of(count, total, bound, lean, full):
    weights = [(1 << 20) // math.isqrt(rank ** lean) + 1 for rank in range(1, count + 1)]
    largest = bound if full else min(bound, max(-(-total // count), total * weights[0] // sum(weights)))
    least = 1 if total - largest >= count - 1 else 0
    counts, surplus = [largest] + [least] * (count - 1), total - largest - least * (count - 1)
    while surplus > 0:
        candidates = [i for i in range(1, count) if counts[i] < largest] or [i for i in range(1, count) if counts[i] < bound]
        pool, budget = sum([weights[i] for i in candidates]), surplus
        for i in candidates:
            addition = min(bound - counts[i], max(1, budget * weights[i] // pool), surplus)
            counts[i] = counts[i] + addition
            surplus = surplus - addition
    return np.array(counts)


def centred(own_key, shape, spread, bound, cuts=(), kind=jnp.bfloat16):
    values = jax.random.normal(own_key, shape, jnp.float32) * spread
    if len(cuts) > 0:
        values = block_levels(own_key, shape, cuts, -0.22, 0.18) * values
    return jnp.clip(values, min=-bound, max=bound).astype(kind)


def setup_inputs(seed: int = 0) -> dict:
    streams_of = jax.random.split(jax.random.key(seed), 20)
    block_in = centred(streams_of[0], (TOKENS, MODEL_WIDTH), 1.0, 6.0, ((0, 32),), jnp.float32)
    cotangent = centred(streams_of[1], (TOKENS, MODEL_WIDTH), 1.0, 6.0, ((0, 32),), jnp.float32)
    routes_keys = jax.random.split(jax.random.fold_in(streams_of[2], 1), TOKENS // (SEQS * SEQ))
    routes_turns = jax.random.permutation(jax.random.fold_in(streams_of[2], 3), TOKENS // (SEQS * SEQ))
    routes = jax.vmap(lambda own, number: deal_out(jax.random.fold_in(streams_of[2], 2), own, number, SEQS * SEQ, E, TOPK, CAP, 0))(routes_keys, routes_turns).reshape((TOKENS, TOPK))
    gate_weights = jnp.clip(0.02 + 0.28 * jax.random.uniform(streams_of[3], (TOKENS, TOPK), jnp.float32) ** block_levels(streams_of[3], (TOKENS, TOPK), ((0, 8),), -0.2, 0.2), 0.02, 0.3)
    norm_gains = jnp.clip(1.0 + 0.1 * jax.random.normal(streams_of[4], (2, MODEL_WIDTH), jnp.float32), 0.5, 1.5)
    attention_weight = centred(streams_of[5], (4, MODEL_WIDTH, KEY_VALUE_HEADS * HEAD_SIZE), MODEL_WIDTH ** -0.5, 0.1875, ((1, 8), (2, 4)), jnp.float32)
    output_weight = centred(streams_of[6], (2, MODEL_WIDTH, KEY_VALUE_HEADS * HEAD_SIZE), (QUERY_HEADS * HEAD_SIZE // 16) ** -0.5, 0.75, ((1, 8), (2, 4)), jnp.float32)
    w_gate_up = centred(streams_of[7], (E, 2, MODEL_WIDTH, FF), MODEL_WIDTH ** -0.5, 0.1875, ((2, 8), (3, 4)), jnp.float32)
    w_down = centred(streams_of[8], (E, MODEL_WIDTH, FF), (FF // 8) ** -0.5, 0.75, ((1, 8), (2, 4)), jnp.float32)
    m_gains = centred(streams_of[9], (2, MODEL_WIDTH), 20.0, 128.0, ((1, 8),), jnp.float32)
    v_gains = jnp.clip(jnp.exp(math.log(10000.0) - 4.6051702 * jax.random.uniform(streams_of[10], (2, MODEL_WIDTH), jnp.float32) ** block_levels(streams_of[10], (2, MODEL_WIDTH), ((1, 8),), -0.2, 0.2)), 100.0, 10000.0)
    attention_first_moment = centred(streams_of[11], (4, MODEL_WIDTH, KEY_VALUE_HEADS * HEAD_SIZE), 2.0, 12.0, ((1, 8), (2, 4)), jnp.float32)
    attention_second_moment = jnp.clip(jnp.exp(math.log(100.0) - 4.6051702 * jax.random.uniform(streams_of[12], (4, MODEL_WIDTH, KEY_VALUE_HEADS * HEAD_SIZE), jnp.float32) ** block_levels(streams_of[12], (4, MODEL_WIDTH, KEY_VALUE_HEADS * HEAD_SIZE), ((1, 8), (2, 4)), -0.2, 0.2)), 1.0, 100.0)
    output_first_moment = centred(streams_of[13], (2, MODEL_WIDTH, KEY_VALUE_HEADS * HEAD_SIZE), 3.0, 16.0, ((1, 8), (2, 4)), jnp.float32)
    output_second_moment = jnp.clip(jnp.exp(math.log(100.0) - 4.6051702 * jax.random.uniform(streams_of[14], (2, MODEL_WIDTH, KEY_VALUE_HEADS * HEAD_SIZE), jnp.float32) ** block_levels(streams_of[14], (2, MODEL_WIDTH, KEY_VALUE_HEADS * HEAD_SIZE), ((1, 8), (2, 4)), -0.2, 0.2)), 1.0, 100.0)
    m_gate_up = centred(streams_of[15], (E, 2, MODEL_WIDTH, FF), 5.0, 32.0, ((2, 8), (3, 4)), jnp.float32)
    v_gate_up = jnp.clip(jnp.exp(math.log(1000.0) - 4.6051702 * jax.random.uniform(streams_of[16], (E, 2, MODEL_WIDTH, FF), jnp.float32) ** block_levels(streams_of[16], (E, 2, MODEL_WIDTH, FF), ((2, 8), (3, 4)), -0.2, 0.2)), 10.0, 1000.0)
    m_down = centred(streams_of[17], (E, MODEL_WIDTH, FF), 2.0, 12.0, ((1, 8), (2, 4)), jnp.float32)
    v_down = jnp.clip(jnp.exp(math.log(100.0) - 4.6051702 * jax.random.uniform(streams_of[18], (E, MODEL_WIDTH, FF), jnp.float32) ** block_levels(streams_of[18], (E, MODEL_WIDTH, FF), ((1, 8), (2, 4)), -0.2, 0.2)), 1.0, 100.0)
    return {"block_in": block_in, "cotangent": cotangent, "routes": routes, "gate_weights": gate_weights, "norm_gains": norm_gains, "attention_weight": attention_weight, "output_weight": output_weight, "w_gate_up": w_gate_up, "w_down": w_down, "m_gains": m_gains, "v_gains": v_gains, "attention_first_moment": attention_first_moment, "attention_second_moment": attention_second_moment, "output_first_moment": output_first_moment, "output_second_moment": output_second_moment, "m_gate_up": m_gate_up, "v_gate_up": v_gate_up, "m_down": m_down, "v_down": v_down}


norm_eps = 1e-05
beta_one = 0.9
beta_two = 0.95
adam_eps = 1e-08
rate_matrix = 0.02
rate_gain = 0.2
decay_matrix = 0.1
rope_base = 10000.0

def product(form, left, right):
    return jnp.einsum(form, left.astype(jnp.float32), right.astype(jnp.float32), precision=lax.Precision.HIGHEST)

def rope_tables(length, width):
    half_width = width // 2
    frequency = rope_base ** (-(2.0 * jnp.arange(half_width, dtype=jnp.float32)) / width)
    angles = jnp.arange(length, dtype=jnp.float32)[:, None] * frequency[None, :]
    return (jnp.cos(angles)[:, None, :], jnp.sin(angles)[:, None, :])

def rotate(vectors, cos_table, sine_table):
    half_width = vectors.shape[-1] // 2
    lower_half = vectors[..., :half_width]
    upper_half = vectors[..., half_width:]
    return jnp.concatenate([lower_half * cos_table - upper_half * sine_table, upper_half * cos_table + lower_half * sine_table], axis=-1)

def unrotate(vectors, cos_table, sine_table):
    half_width = vectors.shape[-1] // 2
    lower_half = vectors[..., :half_width]
    upper_half = vectors[..., half_width:]
    return jnp.concatenate([lower_half * cos_table + upper_half * sine_table, upper_half * cos_table - lower_half * sine_table], axis=-1)

def causal_scores(queries, keys_rot):
    scale = queries.shape[-1] ** (-0.5)
    scores = product('jqgh,kgh->jgqk', queries, keys_rot) * scale
    length = scores.shape[-1]
    allowed = lax.broadcasted_iota(jnp.int32, (length, length), 0) >= lax.broadcasted_iota(jnp.int32, (length, length), 1)
    return jnp.where(allowed, scores, -jnp.inf)

def attend(items):
    queries, keys_rot, values = items
    scores = causal_scores(queries, keys_rot)
    log_totals = jax.nn.logsumexp(scores, axis=-1)
    softmax_b = jnp.exp(scores - log_totals[..., None]).astype(jnp.bfloat16)
    attended = product('jgqk,kgh->jqgh', softmax_b, values).astype(jnp.bfloat16)
    return (attended, log_totals)

def attend_back(items):
    queries, keys_rot, values, attended, log_totals, attended_cot = items
    scale = queries.shape[-1] ** (-0.5)
    scores = causal_scores(queries, keys_rot)
    softmax_f = jnp.exp(scores - log_totals[..., None])
    softmax_b = softmax_f.astype(jnp.bfloat16)
    value_cot = product('jgqk,jqgh->kgh', softmax_b, attended_cot)
    weight_cot = product('jqgh,kgh->jgqk', attended_cot, values)
    row_dots = product('jqgh,jqgh->jgq', attended_cot, attended)
    score_cot = (softmax_f * (weight_cot - row_dots[..., None])).astype(jnp.bfloat16)
    query_cot = product('jgqk,kgh->jqgh', score_cot, keys_rot) * scale
    key_cot = product('jgqk,jqgh->kgh', score_cot, queries) * scale
    return (query_cot, key_cot, value_cot)

def slot_table(route_rows, gate_rows, tok_count):
    hits = (route_rows[:, :, None] == jnp.arange(E, dtype=jnp.int32)[None, None, :]).astype(jnp.int32)
    per_token = lax.optimization_barrier(jnp.sum(hits, axis=1, dtype=jnp.int32))
    before = jnp.cumsum(per_token, axis=0, dtype=jnp.int32) - per_token
    position = lax.optimization_barrier(jnp.sum(hits * before[:, None, :], axis=2, dtype=jnp.int32))
    flat_slot = (route_rows * CAP + position).reshape(-1).astype(jnp.int32)
    owner = jnp.broadcast_to(jnp.arange(tok_count, dtype=jnp.int32)[:, None], route_rows.shape).reshape(-1)
    slot_token = jnp.full((E * CAP,), tok_count, jnp.int32).at[flat_slot].set(owner)
    slot_weight = jnp.zeros((E * CAP,), jnp.float32).at[flat_slot].set(gate_rows.reshape(-1))
    return (slot_token, slot_weight)

def group_pass(block_rows, cot_rows, route_rows, gate_rows, gains_b, attn_b, out_b, gate_up_b, down_b, cos_table, sine_table):
    tok_count = block_rows.shape[0]
    seq_count = tok_count // SEQ
    width = block_rows.shape[1]
    kv_count = attn_b.shape[2] // HEAD_SIZE
    gain_one = gains_b[0].astype(jnp.float32)
    gain_two = gains_b[1].astype(jnp.float32)
    inv_one = lax.rsqrt(lax.optimization_barrier(jnp.mean(block_rows * block_rows, axis=1, keepdims=True)) + norm_eps)
    normed_one = (block_rows * inv_one * gain_one).astype(jnp.bfloat16)
    projected = product('td,zdc->ztc', normed_one, attn_b)
    head_vals = projected.reshape(4, seq_count, SEQ, kv_count, HEAD_SIZE)
    queries = rotate(head_vals[0:2], cos_table, sine_table).astype(jnp.bfloat16).transpose(1, 0, 2, 3, 4)
    keys_rot = rotate(head_vals[2], cos_table, sine_table).astype(jnp.bfloat16)
    values = head_vals[3].astype(jnp.bfloat16)
    attended, log_totals = lax.map(attend, (queries, keys_rot, values))
    attended_flat = attended.transpose(1, 0, 2, 3, 4).reshape(2, tok_count, kv_count * HEAD_SIZE)
    residual = block_rows + product('jtc,jdc->td', attended_flat, out_b)
    inv_two = lax.rsqrt(lax.optimization_barrier(jnp.mean(residual * residual, axis=1, keepdims=True)) + norm_eps)
    normed_two = (residual * inv_two * gain_two).astype(jnp.bfloat16)
    slot_token, slot_weight = slot_table(route_rows, gate_rows, tok_count)
    padded = jnp.concatenate([normed_two, jnp.zeros((1, width), jnp.bfloat16)], axis=0)
    expert_in = padded[slot_token].reshape(E, CAP, width)
    gate_up = product('ecd,ezdf->zecf', expert_in, gate_up_b)
    gate_vals = gate_up[0]
    up_vals = gate_up[1]
    hidden = (jax.nn.silu(gate_vals) * up_vals).astype(jnp.bfloat16)
    expert_out = product('ecf,edf->ecd', hidden, down_b)
    mixture = jnp.zeros((tok_count + 1, width), jnp.float32).at[slot_token].add(expert_out.reshape(E * CAP, width) * slot_weight[:, None])
    block_out = residual + mixture[:tok_count]
    cot_pad = jnp.concatenate([cot_rows, jnp.zeros((1, width), jnp.float32)], axis=0)
    slot_cot = (slot_weight[:, None] * cot_pad[slot_token]).astype(jnp.bfloat16).reshape(E, CAP, width)
    grad_down = product('ecd,ecf->edf', slot_cot, hidden)
    hidden_cot = product('ecd,edf->ecf', slot_cot, down_b)
    sigmoid_vals = jax.nn.sigmoid(gate_vals)
    gate_cot = (hidden_cot * up_vals * sigmoid_vals * (1.0 + gate_vals * (1.0 - sigmoid_vals))).astype(jnp.bfloat16)
    up_cot = (hidden_cot * gate_vals * sigmoid_vals).astype(jnp.bfloat16)
    both_cot = jnp.stack([gate_cot, up_cot])
    grad_gate_up = product('ecd,zecf->ezdf', expert_in, both_cot)
    input_cot = product('zecf,ezdf->ecd', both_cot, gate_up_b)
    normed_two_cot = jnp.zeros((tok_count + 1, width), jnp.float32).at[slot_token].add(input_cot.reshape(E * CAP, width))[:tok_count]
    scaled_two = gain_two * normed_two_cot
    residual_cot = cot_rows + inv_two * scaled_two - residual * inv_two ** 3 * lax.optimization_barrier(jnp.mean(scaled_two * residual, axis=1, keepdims=True))
    resid_cot_b = residual_cot.astype(jnp.bfloat16)
    grad_out = product('td,jtc->jdc', resid_cot_b, attended_flat)
    attended_cot = product('td,jdc->jtc', resid_cot_b, out_b).astype(jnp.bfloat16)
    attended_cot = attended_cot.reshape(2, seq_count, SEQ, kv_count, HEAD_SIZE).transpose(1, 0, 2, 3, 4)
    query_cot, key_cot, value_cot = lax.map(attend_back, (queries, keys_rot, values, attended, log_totals, attended_cot))
    query_plain = unrotate(query_cot, cos_table, sine_table).transpose(1, 0, 2, 3, 4).reshape(2, tok_count, kv_count * HEAD_SIZE)
    key_plain = unrotate(key_cot, cos_table, sine_table).reshape(1, tok_count, kv_count * HEAD_SIZE)
    proj_cot = jnp.concatenate([query_plain, key_plain, value_cot.reshape(1, tok_count, kv_count * HEAD_SIZE)], axis=0).astype(jnp.bfloat16)
    grad_attn = product('td,ztc->zdc', normed_one, proj_cot)
    normed_one_cot = product('ztc,zdc->td', proj_cot, attn_b)
    scaled_one = gain_one * normed_one_cot
    input_grad = residual_cot + inv_one * scaled_one - block_rows * inv_one ** 3 * lax.optimization_barrier(jnp.mean(scaled_one * block_rows, axis=1, keepdims=True))
    grad_gains = jnp.stack([lax.optimization_barrier(jnp.sum(normed_one_cot * block_rows * inv_one, axis=0)), lax.optimization_barrier(jnp.sum(normed_two_cot * residual * inv_two, axis=0))])
    return (block_out, input_grad, (grad_gains, grad_attn, grad_out, grad_gate_up, grad_down))

def adamw_update(weight, moment_one, moment_two, gradient, rate, decay):
    new_one = beta_one * moment_one + (1.0 - beta_one) * gradient
    new_two = beta_two * moment_two + (1.0 - beta_two) * gradient * gradient
    corrected_one = new_one / (1.0 - beta_one ** STEP)
    corrected_two = new_two / (1.0 - beta_two ** STEP)
    new_weight = weight - rate * (corrected_one / (jnp.sqrt(corrected_two) + adam_eps) + decay * weight)
    return (new_weight, new_one, new_two)

def reference(block_in, cotangent, routes, gate_weights, norm_gains, attention_weight, output_weight, w_gate_up, w_down, m_gains, v_gains, attention_first_moment, attention_second_moment, output_first_moment, output_second_moment, m_gate_up, v_gate_up, m_down, v_down):
    masters = (norm_gains, attention_weight, output_weight, w_gate_up, w_down)
    gains_b, attn_b, out_b, gate_up_b, down_b = [weight.astype(jnp.bfloat16) for weight in masters]
    cos_table, sine_table = rope_tables(SEQ, HEAD_SIZE)
    width = block_in.shape[1]
    group_tokens = SEQS * SEQ
    pieces = (block_in.reshape(N_DP, group_tokens, width), cotangent.reshape(N_DP, group_tokens, width), routes.reshape(N_DP, group_tokens, TOPK), gate_weights.reshape(N_DP, group_tokens, TOPK))
    initial = tuple((jnp.zeros(weight.shape, jnp.float32) for weight in masters))

    def one_group(totals, items):
        block_rows, cot_rows, route_rows, gate_rows = items
        block_part, grad_part, gradients = group_pass(block_rows, cot_rows, route_rows, gate_rows, gains_b, attn_b, out_b, gate_up_b, down_b, cos_table, sine_table)
        return (tuple((total + gradient for total, gradient in zip(totals, gradients))), (block_part, grad_part))
    totals, (block_parts, grad_parts) = lax.scan(one_group, initial, pieces)
    block_out = block_parts.reshape(-1, width)
    input_grad = grad_parts.reshape(-1, width)
    grad_gains, grad_attn, grad_out, grad_gate_up, grad_down = totals
    new_gains, new_m_gains, new_v_gains = adamw_update(norm_gains, m_gains, v_gains, grad_gains, rate_gain, 0.0)
    new_attn, new_m_attn, new_v_attn = adamw_update(attention_weight, attention_first_moment, attention_second_moment, grad_attn, rate_matrix, decay_matrix)
    new_out, new_m_out, new_v_out = adamw_update(output_weight, output_first_moment, output_second_moment, grad_out, rate_matrix, decay_matrix)
    new_gate_up, new_m_gate_up, new_v_gate_up = adamw_update(w_gate_up, m_gate_up, v_gate_up, grad_gate_up, rate_matrix, decay_matrix)
    new_down, new_m_down, new_v_down = adamw_update(w_down, m_down, v_down, grad_down, rate_matrix, decay_matrix)
    return (block_out, input_grad, grad_gains, grad_attn, grad_out, grad_gate_up, grad_down, new_gains, new_attn, new_out, new_gate_up, new_down, new_m_gains, new_v_gains, new_m_attn, new_v_attn, new_m_out, new_v_out, new_m_gate_up, new_v_gate_up, new_m_down, new_v_down)
```

```python
import functools

import jax
import jax.numpy as jnp
from jax import lax
from jax.experimental import pallas as pl
from jax.experimental.pallas import tpu as pltpu
from jax.sharding import PartitionSpec as P


HEAD_SIZE = 64
SEQ = 512
STEP = 3


norm_eps = 1e-05
beta_one = 0.9
beta_two = 0.95
adam_eps = 1e-08
rate_matrix = 0.02
rate_gain = 0.2
decay_matrix = 0.1
rope_base = 10000.0


def rope_tables(count, cols):
    half_width = HEAD_SIZE // 2
    frequency = rope_base ** (-(2.0 * jnp.arange(half_width, dtype=jnp.float32)) / HEAD_SIZE)
    positions = (jnp.arange(count) % SEQ).astype(jnp.float32)
    angles = positions[:, None] * frequency[None, :]
    cosines = jnp.cos(angles)
    sines = jnp.sin(angles)
    heads = cols // HEAD_SIZE
    return (
        jnp.tile(jnp.concatenate([cosines, cosines], axis=1), (1, heads)),
        jnp.tile(jnp.concatenate([-sines, sines], axis=1), (1, heads)),
    )


def adamw_update(weight, moment_one, moment_two, gradient, rate, decay):
    new_one = beta_one * moment_one + (1.0 - beta_one) * gradient
    new_two = beta_two * moment_two + (1.0 - beta_two) * gradient * gradient
    corrected_one = new_one / (1.0 - beta_one**STEP)
    corrected_two = new_two / (1.0 - beta_two**STEP)
    new_weight = weight - rate * (
        corrected_one / (jnp.sqrt(corrected_two) + adam_eps) + decay * weight
    )
    return (new_weight, new_one, new_two)


def exchange(block, axis, step):
    count = lax.axis_size(axis)
    return lax.ppermute(block, axis, [(i, i ^ step) for i in range(count)])


MESH_ID = pl.DeviceIdType.MESH


def rolled(vectors, sine_table):
    width = vectors.shape[1]
    half_width = HEAD_SIZE // 2
    lane = lax.broadcasted_iota(jnp.int32, vectors.shape, 1)
    ahead = pltpu.roll(vectors, width - half_width, 1)
    behind = pltpu.roll(vectors, half_width, 1)
    return jnp.where(lane % HEAD_SIZE < half_width, ahead, behind) * sine_table


def causal_mask(count):
    row = lax.broadcasted_iota(jnp.int32, (count, count), 0)
    column = lax.broadcasted_iota(jnp.int32, (count, count), 1)
    allowed = row >= column
    if count > SEQ:
        allowed = allowed & (row // SEQ == column // SEQ)
    return allowed


def dot_last(left, right):
    return lax.dot_general(
        left, right, (((1,), (1,)), ((), ())), preferred_element_type=jnp.float32
    )


def dot_first(left, right):
    return lax.dot_general(
        left, right, (((0,), (0,)), ((), ())), preferred_element_type=jnp.float32
    )


class Links:
    def __init__(self, dp_count, z_count):
        self.dp_count = dp_count
        self.z_count = z_count
        self.me = lax.axis_index("dp")
        self.z = lax.axis_index("tensor")
        self.sibling = self.me + 1 - 2 * (self.me % 2)
        self.sent = []

    def barrier(self):
        semaphore = pltpu.get_barrier_semaphore()
        peers = [((self.me + s) % self.dp_count, self.z) for s in range(1, self.dp_count)]
        peers += [(self.me, (self.z + s) % self.z_count) for s in range(1, self.z_count)]
        for peer in peers:
            pl.semaphore_signal(semaphore, inc=1, device_id=peer, device_id_type=MESH_ID)
        pl.semaphore_wait(semaphore, len(peers))

    def send(self, source, target, send_sem, recv_sem, device):
        copy = pltpu.make_async_remote_copy(
            src_ref=source,
            dst_ref=target,
            send_sem=send_sem,
            recv_sem=recv_sem,
            device_id=device,
            device_id_type=MESH_ID,
        )
        copy.start()
        self.sent.append(copy)
        return copy

    def dp_peers(self):
        return [(s, (self.me + s) % self.dp_count) for s in range(1, self.dp_count)]

    def z_peers(self):
        order = sorted(range(1, self.z_count), key=lambda s: abs(s - self.z_count // 2))
        return [(s, (self.z + s) % self.z_count) for s in order]

    def z_gather(self, ref, sems):
        return [
            self.send(
                ref.at[self.z], ref.at[self.z], sems.at[0, s], sems.at[1, s], (self.me, p)
            )
            for s, p in self.z_peers()
        ]

    def z_scatter(self, ref, land, sems):
        return [
            self.send(ref.at[p], land.at[self.z], sems.at[0, s], sems.at[1, s], (self.me, p))
            for s, p in self.z_peers()
        ]

    def z_sources(self):
        return [(self.z + self.z_count - s) % self.z_count for s, _ in self.z_peers()]

    def finish(self):
        for copy in self.sent:
            copy.wait_send()


def forward_kernel(
    dp_count,
    z_count,
    block_in,
    cotangent,
    gains_wide,
    attn_rows,
    expert_rows,
    cos_table,
    sine_table,
    residual,
    tokens_pair,
    cot_pair,
    whole_rows,
    attn_all,
    gains_all,
    tokens_one,
    rotated,
    attended,
    log_totals,
    gains_land,
    part,
    land,
    gain_sems,
    attn_sems,
    expert_sems,
    one_sems,
    cot_sems,
    land_sems,
    two_sems,
    pair_sems,
    own_sem,
):
    bf = jnp.bfloat16
    f32 = jnp.float32
    net = Links(dp_count, z_count)
    me, z, sibling = net.me, net.z, net.sibling
    own_rows, width = block_in.shape
    tok_count = z_count * own_rows
    cols = attn_rows.shape[1] // 6
    net.barrier()
    gain_copies = [
        net.send(gains_wide, gains_land.at[me], gain_sems.at[0, s], gain_sems.at[1, s], (p, z))
        for s, p in net.dp_peers()
    ]
    attn_copies = [
        net.send(attn_rows, attn_all.at[me], attn_sems.at[0, s], attn_sems.at[1, s], (p, z))
        for s, p in net.dp_peers()
    ]
    cot_pair[0, z] = cotangent[...].astype(bf)
    attn_all[me] = attn_rows[...]
    gains_land[me] = gains_wide[...]
    block = block_in[...]
    inv_one = lax.rsqrt(jnp.mean(block * block, axis=1, keepdims=True) + norm_eps)
    for copy in gain_copies:
        copy.wait_recv()
    gains = gains_land[0]
    for i in range(1, dp_count):
        gains = gains + gains_land[i]
    gains_all[...] = gains
    tokens_one[z] = (block * inv_one * gains[0:1]).astype(bf)
    one_copies = net.z_gather(tokens_one, one_sems)
    expert_copies = [
        net.send(
            expert_rows.at[p % 2],
            whole_rows.at[me],
            expert_sems.at[0, s],
            expert_sems.at[1, s],
            (p, z),
        )
        for s, p in net.dp_peers()
    ]
    own_copy = pltpu.make_async_copy(expert_rows.at[me % 2], whole_rows.at[me], own_sem)
    own_copy.start()

    def to_sibling(ref, index, slot):
        return net.send(
            ref.at[0, index],
            ref.at[1, index],
            pair_sems.at[0, slot],
            pair_sems.at[1, slot],
            (sibling, z),
        )

    pair_copies = []
    for copy in one_copies + attn_copies:
        copy.wait_recv()
    cot_copies = net.z_gather(cot_pair.at[0], cot_sems)
    pair_copies.append(to_sibling(cot_pair, z, 0))
    weights = attn_all[...].reshape(dp_count * attn_rows.shape[0], 6 * cols)
    tokens = tokens_one[...].reshape(tok_count, width)
    projected = jnp.dot(tokens, weights[:, : 4 * cols], preferred_element_type=f32)
    cosines = cos_table[...]
    sines = sine_table[...]
    for i in range(3):
        vectors = projected[:, i * cols : (i + 1) * cols]
        rotated[:, i * cols : (i + 1) * cols] = (
            vectors * cosines + rolled(vectors, sines)
        ).astype(bf)
    rotated[:, 3 * cols :] = projected[:, 3 * cols :].astype(bf)
    allowed = causal_mask(tok_count)
    scale = HEAD_SIZE ** (-0.5)
    totals = []
    for j in range(2):
        heads = []
        for g in range(cols // HEAD_SIZE):
            at = g * HEAD_SIZE
            query = rotated[:, j * cols + at : j * cols + at + HEAD_SIZE]
            key = rotated[:, 2 * cols + at : 2 * cols + at + HEAD_SIZE]
            value = rotated[:, 3 * cols + at : 3 * cols + at + HEAD_SIZE]
            scores = jnp.where(allowed, dot_last(query, key) * scale, -1e30)
            top = jnp.max(scores, axis=1, keepdims=True)
            total = top + jnp.log(jnp.sum(jnp.exp(scores - top), axis=1, keepdims=True))
            softmax = jnp.exp(scores - total).astype(bf)
            heads.append(jnp.dot(softmax, value, preferred_element_type=f32).astype(bf))
            totals.append(total)
        attended[:, j * cols : (j + 1) * cols] = jnp.concatenate(heads, axis=1)
    for i, total in enumerate(totals):
        log_totals[i] = total
    partial_value = dot_last(attended[...], weights[:, 4 * cols :])
    part[...] = partial_value.astype(bf).reshape(z_count, own_rows, width)
    land_copies = net.z_scatter(part, land, land_sems)
    for i, (copy, source) in enumerate(zip(cot_copies, net.z_sources())):
        copy.wait_recv()
        pair_copies.append(to_sibling(cot_pair, source, 1 + i))
    for copy in land_copies:
        copy.wait_recv()
    total = block + part[z].astype(f32)
    for source in net.z_sources():
        total = total + land[source].astype(f32)
    residual[...] = total
    inv_two = lax.rsqrt(jnp.mean(total * total, axis=1, keepdims=True) + norm_eps)
    tokens_pair[0, z] = (total * inv_two * gains[1:2]).astype(bf)
    two_copies = net.z_gather(tokens_pair.at[0], two_sems)
    pair_copies.append(to_sibling(tokens_pair, z, z_count))
    for i, (copy, source) in enumerate(zip(two_copies, net.z_sources())):
        copy.wait_recv()
        pair_copies.append(to_sibling(tokens_pair, source, z_count + 1 + i))
    for copy in pair_copies + expert_copies:
        copy.wait_recv()
    own_copy.wait()
    net.finish()


def backward_kernel(
    dp_count,
    z_count,
    back,
    mixture,
    grads,
    residual_in,
    cotangent,
    block_in,
    gains_all,
    tokens_one,
    rotated,
    attended,
    log_totals,
    attn_all,
    cos_table,
    sine_table,
    grads_land,
    attn_land,
    block_out,
    input_grad,
    back_land,
    mix_land,
    part,
    land,
    resid_all,
    norm_part,
    norm_land,
    mix_part,
    mix_sum_land,
    attn_local,
    grad_sems,
    attn_sems,
    pair_sems,
    land_sems,
    resid_sems,
    norm_sems,
    mix_sems,
    own_sem,
):
    bf = jnp.bfloat16
    f32 = jnp.float32
    net = Links(dp_count, z_count)
    me, z, sibling = net.me, net.z, net.sibling
    own_rows, width = block_in.shape
    tok_count = z_count * own_rows
    rows = attn_all.shape[1]
    cols = attn_all.shape[2] // 6
    net.barrier()
    back_copy = net.send(
        back.at[1], back_land, pair_sems.at[0, 0], pair_sems.at[1, 0], (sibling, z)
    )
    mix_copy = net.send(
        mixture.at[1], mix_land, pair_sems.at[0, 1], pair_sems.at[1, 1], (sibling, z)
    )
    grad_copies = [
        net.send(
            grads.at[p], grads_land.at[me], grad_sems.at[0, s], grad_sems.at[1, s], (p, z)
        )
        for s, p in net.dp_peers()
    ]
    own_copy = pltpu.make_async_copy(grads.at[me], grads_land.at[me], own_sem)
    own_copy.start()
    back_copy.wait_recv()
    part[...] = (back[0].astype(f32) + back_land[...].astype(f32)).astype(bf)
    land_copies = net.z_scatter(part, land, land_sems)
    mix_copy.wait_recv()
    mix_part[...] = (mixture[0].astype(f32) + mix_land[...].astype(f32)).astype(bf)
    residual = residual_in[...]
    gain_one = gains_all[0:1]
    gain_two = gains_all[1:2]
    inv_two = lax.rsqrt(jnp.mean(residual * residual, axis=1, keepdims=True) + norm_eps)
    for copy in land_copies:
        copy.wait_recv()
    normed_two_cot = part[z].astype(f32)
    for source in net.z_sources():
        normed_two_cot = normed_two_cot + land[source].astype(f32)
    scaled = gain_two * normed_two_cot
    residual_cot = (
        cotangent[...]
        + inv_two * scaled
        - residual
        * (inv_two * inv_two * inv_two * jnp.mean(scaled * residual, axis=1, keepdims=True))
    )
    input_grad[...] = residual_cot
    resid_all[z] = residual_cot.astype(bf)
    resid_copies = net.z_gather(resid_all, resid_sems)
    for copy in resid_copies:
        copy.wait_recv()
    mix_copies = net.z_scatter(mix_part, mix_sum_land, mix_sems)
    weights = attn_all[...].reshape(dp_count * rows, 6 * cols)
    resid = resid_all[...].reshape(tok_count, width)
    attended_cot = jnp.dot(resid, weights[:, 4 * cols :], preferred_element_type=f32).astype(bf)
    allowed = causal_mask(tok_count)
    scale = HEAD_SIZE ** (-0.5)
    heads = cols // HEAD_SIZE
    query_cots = [[None] * heads for _ in range(2)]
    key_cots = [None] * heads
    value_cots = [None] * heads
    for g in range(heads):
        at = g * HEAD_SIZE
        key = rotated[:, 2 * cols + at : 2 * cols + at + HEAD_SIZE]
        value = rotated[:, 3 * cols + at : 3 * cols + at + HEAD_SIZE]
        for j in range(2):
            query = rotated[:, j * cols + at : j * cols + at + HEAD_SIZE]
            cot = attended_cot[:, j * cols + at : j * cols + at + HEAD_SIZE]
            seen = attended[:, j * cols + at : j * cols + at + HEAD_SIZE]
            scores = jnp.where(allowed, dot_last(query, key) * scale, -1e30)
            softmax = jnp.exp(scores - log_totals[j * heads + g])
            dots = jnp.sum(cot.astype(f32) * seen.astype(f32), axis=1, keepdims=True)
            score_cot = (softmax * (dot_last(cot, value) - dots)).astype(bf)
            value_cot = dot_first(softmax.astype(bf), cot)
            key_cot = dot_first(score_cot, query) * scale
            query_cots[j][g] = jnp.dot(score_cot, key, preferred_element_type=f32) * scale
            value_cots[g] = value_cot if j == 0 else value_cots[g] + value_cot
            key_cots[g] = key_cot if j == 0 else key_cots[g] + key_cot
    cosines = cos_table[...]
    sines = sine_table[...]

    def unrotated(parts):
        vectors = jnp.concatenate(parts, axis=1)
        return (vectors * cosines - rolled(vectors, sines)).astype(bf)

    proj_cot = jnp.concatenate(
        [
            unrotated(query_cots[0]),
            unrotated(query_cots[1]),
            unrotated(key_cots),
            jnp.concatenate(value_cots, axis=1).astype(bf),
        ],
        axis=1,
    )
    norm_terms = dot_last(proj_cot, weights[:, : 4 * cols])
    norm_part[...] = norm_terms.astype(bf).reshape(z_count, own_rows, width)
    norm_copies = net.z_scatter(norm_part, norm_land, norm_sems)
    tokens = tokens_one[...].reshape(tok_count, width)
    attn_local[:, :, : 4 * cols] = (
        dot_first(tokens, proj_cot).astype(bf).reshape(dp_count, rows, 4 * cols)
    )
    attn_local[:, :, 4 * cols :] = (
        dot_first(resid, attended[...]).astype(bf).reshape(dp_count, rows, 2 * cols)
    )
    attn_copies = [
        net.send(
            attn_local.at[p], attn_land.at[me], attn_sems.at[0, s], attn_sems.at[1, s], (p, z)
        )
        for s, p in net.dp_peers()
    ]
    attn_land[me] = attn_local[me]
    for copy in mix_copies:
        copy.wait_recv()
    total = residual + mix_part[z].astype(f32)
    for source in net.z_sources():
        total = total + mix_sum_land[source].astype(f32)
    block_out[...] = total
    block = block_in[...]
    inv_one = lax.rsqrt(jnp.mean(block * block, axis=1, keepdims=True) + norm_eps)
    for copy in norm_copies:
        copy.wait_recv()
    normed_one_cot = norm_part[z].astype(f32)
    for source in net.z_sources():
        normed_one_cot = normed_one_cot + norm_land[source].astype(f32)
    scaled = gain_one * normed_one_cot
    input_grad[...] = (
        input_grad[...]
        + inv_one * scaled
        - block * (inv_one * inv_one * inv_one * jnp.mean(scaled * block, axis=1, keepdims=True))
    )
    for copy in attn_copies + grad_copies:
        copy.wait_recv()
    own_copy.wait()
    net.finish()


def in_vmem(count):
    return [pl.BlockSpec(memory_space=pltpu.VMEM)] * count


def in_place(count):
    return [pl.BlockSpec(memory_space=pl.ANY)] * count


def local(
    block_in,
    cotangent,
    routes,
    gate_weights,
    norm_gains,
    attention_weight,
    output_weight,
    w_gate_up,
    w_down,
    m_gains,
    v_gains,
    attention_first_moment,
    attention_second_moment,
    output_first_moment,
    output_second_moment,
    m_gate_up,
    v_gate_up,
    m_down,
    v_down,
):
    bf = jnp.bfloat16
    f32 = jnp.float32
    tok_count = routes.shape[0]
    own_rows, width = block_in.shape
    experts = w_gate_up.shape[0]
    rows = w_gate_up.shape[2]
    units = w_gate_up.shape[3]
    cols = attention_weight.shape[2]
    dp_count = lax.axis_size("dp")
    z_count = lax.axis_size("tensor")
    me = lax.axis_index("dp")
    parity = me % 2
    held = experts // 2
    half = held * units
    shape = jax.ShapeDtypeStruct
    dma = pltpu.SemaphoreType.DMA
    block_of = (z_count, own_rows, width)

    attn_rows = jnp.concatenate([attention_weight, output_weight], axis=0)
    attn_rows = attn_rows.astype(bf).transpose(1, 0, 2).reshape(rows, 6 * cols)
    gate_up_b = w_gate_up.astype(bf)
    down_b = w_down.astype(bf)
    expert_rows = jnp.concatenate([gate_up_b, down_b[:, None]], axis=1)
    expert_rows = (
        expert_rows.reshape(2, held, 3, rows, units)
        .transpose(0, 3, 2, 1, 4)
        .reshape(2, rows, 3 * half)
    )
    gains_wide = lax.dynamic_update_slice_in_dim(
        jnp.zeros((2, width), f32), norm_gains.astype(bf).astype(f32), me * rows, axis=1
    )
    cos_table, sine_table = rope_tables(tok_count, cols)

    (
        residual,
        tokens_pair,
        cot_pair,
        whole_rows,
        attn_all,
        gains_all,
        tokens_one,
        rotated,
        attended,
        log_totals,
    ) = pl.pallas_call(
        functools.partial(forward_kernel, dp_count, z_count),
        out_shape=(
            shape((own_rows, width), f32),
            shape((2,) + block_of, bf),
            shape((2,) + block_of, bf),
            shape((dp_count, rows, 3 * half), bf),
            shape((dp_count, rows, 6 * cols), bf),
            shape((2, width), f32),
            shape(block_of, bf),
            shape((tok_count, 4 * cols), bf),
            shape((tok_count, 2 * cols), bf),
            shape((2 * cols // HEAD_SIZE, tok_count, 1), f32),
        ),
        in_specs=in_vmem(4) + in_place(1) + in_vmem(2),
        out_specs=in_vmem(3) + in_place(1) + in_vmem(6),
        scratch_shapes=[
            pltpu.VMEM((dp_count, 2, width), f32),
            pltpu.VMEM(block_of, bf),
            pltpu.VMEM(block_of, bf),
            dma((2, dp_count)),
            dma((2, dp_count)),
            dma((2, dp_count)),
            dma((2, z_count)),
            dma((2, z_count)),
            dma((2, z_count)),
            dma((2, z_count)),
            dma((2, 2 * z_count)),
            dma,
        ],
        compiler_params=pltpu.CompilerParams(
            collective_id=0, has_side_effects=True, vmem_limit_bytes=48 * 1024 * 1024
        ),
        name="forward_kernel",
    )(block_in, cotangent, gains_wide, attn_rows, expert_rows, cos_table, sine_table)

    expert_ids = jnp.arange(experts, dtype=jnp.int32)[None, None, :]
    token_weight = jnp.sum(
        jnp.where(routes[:, :, None] == expert_ids, gate_weights[:, :, None], 0.0), axis=1
    )
    token_weight = token_weight.reshape(tok_count, 2, held)
    weight_mine = lax.dynamic_index_in_dim(token_weight, parity, 1, False)
    weight_other = lax.dynamic_index_in_dim(token_weight, 1 - parity, 1, False)
    weight_pair = jnp.concatenate([weight_mine, exchange(weight_other, "dp", 1)], axis=0)
    weight_wide = jnp.broadcast_to(
        weight_pair[:, :, None], (2 * tok_count, held, units)
    ).reshape(2 * tok_count, half)

    tokens_pair = tokens_pair.reshape(2 * tok_count, width)
    cot_pair = cot_pair.reshape(2 * tok_count, width)
    whole_rows = whole_rows.reshape(dp_count * rows, 3 * half)
    gate_up_all = whole_rows[:, : 2 * half]
    down_all = whole_rows[:, 2 * half :]
    gate_up = jnp.dot(tokens_pair, gate_up_all, preferred_element_type=f32)
    gate_vals = gate_up[:, :half]
    up_vals = gate_up[:, half:]
    sigmoid_vals = jax.nn.sigmoid(gate_vals)
    hidden = (gate_vals * sigmoid_vals * up_vals * weight_wide).astype(bf)
    hidden_cot = jnp.dot(cot_pair, down_all, preferred_element_type=f32) * weight_wide
    gate_cot = (
        hidden_cot * up_vals * sigmoid_vals * (1.0 + gate_vals * (1.0 - sigmoid_vals))
    ).astype(bf)
    up_cot = (hidden_cot * gate_vals * sigmoid_vals).astype(bf)
    both_cot = jnp.concatenate([gate_cot, up_cot], axis=1)
    back = dot_last(both_cot, gate_up_all).astype(bf)
    mixture = dot_last(hidden, down_all).astype(bf)
    gate_up_local = dot_first(tokens_pair, both_cot).astype(bf)
    down_local = dot_first(cot_pair, hidden).astype(bf)
    grads_local = jnp.concatenate([gate_up_local, down_local], axis=1)

    grads_land, attn_land, block_out, input_grad = pl.pallas_call(
        functools.partial(backward_kernel, dp_count, z_count),
        out_shape=(
            shape((dp_count, rows, 3 * half), bf),
            shape((dp_count, rows, 6 * cols), bf),
            shape((own_rows, width), f32),
            shape((own_rows, width), f32),
        ),
        in_specs=in_vmem(2) + in_place(1) + in_vmem(11),
        out_specs=in_place(1) + in_vmem(3),
        scratch_shapes=[
            pltpu.VMEM(block_of, bf),
            pltpu.VMEM(block_of, bf),
            pltpu.VMEM(block_of, bf),
            pltpu.VMEM(block_of, bf),
            pltpu.VMEM(block_of, bf),
            pltpu.VMEM(block_of, bf),
            pltpu.VMEM(block_of, bf),
            pltpu.VMEM(block_of, bf),
            pltpu.VMEM(block_of, bf),
            pltpu.VMEM((dp_count, rows, 6 * cols), bf),
            dma((2, dp_count)),
            dma((2, dp_count)),
            dma((2, 2)),
            dma((2, z_count)),
            dma((2, z_count)),
            dma((2, z_count)),
            dma((2, z_count)),
            dma,
        ],
        compiler_params=pltpu.CompilerParams(
            collective_id=1, has_side_effects=True, vmem_limit_bytes=56 * 1024 * 1024
        ),
        name="backward_kernel",
    )(
        back.reshape((2,) + block_of),
        mixture.reshape((2,) + block_of),
        grads_local.reshape(dp_count, rows, 3 * half),
        residual,
        cotangent,
        block_in,
        gains_all,
        tokens_one,
        rotated,
        attended,
        log_totals,
        attn_all,
        cos_table,
        sine_table,
    )

    both_sum = jnp.sum(attn_land.astype(f32), axis=0)
    both_sum = both_sum.reshape(rows, 6, cols).transpose(1, 0, 2)
    grad_attn = both_sum[:4]
    grad_out = both_sum[4:]
    grads_land = grads_land.reshape(dp_count // 2, 2, rows, 3, held, units)
    expert_sum = jnp.sum(grads_land.astype(f32), axis=0)
    expert_sum = expert_sum.transpose(0, 3, 2, 1, 4).reshape(experts, 3, rows, units)
    grad_gate_up = expert_sum[:, :2]
    grad_down = expert_sum[:, 2]
    gain_local = jnp.stack(
        [
            jnp.sum(attention_weight.astype(bf).astype(f32) * grad_attn, axis=(0, 2)),
            jnp.sum(gate_up_b.astype(f32) * grad_gate_up, axis=(0, 1, 3)),
        ]
    )
    gain_sum = gain_local
    for step in range(1, z_count):
        gain_sum = gain_sum + exchange(gain_local, "tensor", step)
    grad_gains = gain_sum / norm_gains.astype(bf).astype(f32)
    new_gains, new_m_gains, new_v_gains = adamw_update(
        norm_gains, m_gains, v_gains, grad_gains, rate_gain, 0.0
    )
    new_attn, new_m_attn, new_v_attn = adamw_update(
        attention_weight,
        attention_first_moment,
        attention_second_moment,
        grad_attn,
        rate_matrix,
        decay_matrix,
    )
    new_out, new_m_out, new_v_out = adamw_update(
        output_weight,
        output_first_moment,
        output_second_moment,
        grad_out,
        rate_matrix,
        decay_matrix,
    )
    new_gate_up, new_m_gate_up, new_v_gate_up = adamw_update(
        w_gate_up, m_gate_up, v_gate_up, grad_gate_up, rate_matrix, decay_matrix
    )
    new_down, new_m_down, new_v_down = adamw_update(
        w_down, m_down, v_down, grad_down, rate_matrix, decay_matrix
    )
    return (
        block_out,
        input_grad,
        grad_gains,
        grad_attn,
        grad_out,
        grad_gate_up,
        grad_down,
        new_gains,
        new_attn,
        new_out,
        new_gate_up,
        new_down,
        new_m_gains,
        new_v_gains,
        new_m_attn,
        new_v_attn,
        new_m_out,
        new_v_out,
        new_m_gate_up,
        new_v_gate_up,
        new_m_down,
        new_v_down,
    )


def solution(mesh):
    return jax.shard_map(
        local,
        mesh=mesh,
        in_specs=(
            P(("dp", "tensor"), None),
            P(("dp", "tensor"), None),
            P("dp", None),
            P("dp", None),
            P(None, "dp"),
            P(None, "dp", "tensor"),
            P(None, "dp", "tensor"),
            P(None, None, "dp", "tensor"),
            P(None, "dp", "tensor"),
            P(None, "dp"),
            P(None, "dp"),
            P(None, "dp", "tensor"),
            P(None, "dp", "tensor"),
            P(None, "dp", "tensor"),
            P(None, "dp", "tensor"),
            P(None, None, "dp", "tensor"),
            P(None, None, "dp", "tensor"),
            P(None, "dp", "tensor"),
            P(None, "dp", "tensor"),
        ),
        out_specs=(
            P(("dp", "tensor"), None),
            P(("dp", "tensor"), None),
            P(None, "dp"),
            P(None, "dp", "tensor"),
            P(None, "dp", "tensor"),
            P(None, None, "dp", "tensor"),
            P(None, "dp", "tensor"),
            P(None, "dp"),
            P(None, "dp", "tensor"),
            P(None, "dp", "tensor"),
            P(None, None, "dp", "tensor"),
            P(None, "dp", "tensor"),
            P(None, "dp"),
            P(None, "dp"),
            P(None, "dp", "tensor"),
            P(None, "dp", "tensor"),
            P(None, "dp", "tensor"),
            P(None, "dp", "tensor"),
            P(None, None, "dp", "tensor"),
            P(None, None, "dp", "tensor"),
            P(None, "dp", "tensor"),
            P(None, "dp", "tensor"),
        ),
        check_vma=False,
    )
```

```python
import functools

import jax
import jax.numpy as jnp
from jax import lax
from jax.experimental import pallas as pl
from jax.experimental.pallas import tpu as pltpu
from jax.sharding import PartitionSpec as P


HEAD_SIZE = 64
SEQ = 512
STEP = 3


norm_eps = 1e-05
beta_one = 0.9
beta_two = 0.95
adam_eps = 1e-08
rate_matrix = 0.02
rate_gain = 0.2
decay_matrix = 0.1
rope_base = 10000.0


def rope_tables(count, cols):
    half_width = HEAD_SIZE // 2
    frequency = rope_base ** (-(2.0 * jnp.arange(half_width, dtype=jnp.float32)) / HEAD_SIZE)
    positions = (jnp.arange(count) % SEQ).astype(jnp.float32)
    angles = positions[:, None] * frequency[None, :]
    cosines = jnp.cos(angles)
    sines = jnp.sin(angles)
    heads = cols // HEAD_SIZE
    return (
        jnp.tile(jnp.concatenate([cosines, cosines], axis=1), (1, heads)),
        jnp.tile(jnp.concatenate([-sines, sines], axis=1), (1, heads)),
    )


def adamw_update(weight, moment_one, moment_two, gradient, rate, decay):
    new_one = beta_one * moment_one + (1.0 - beta_one) * gradient
    new_two = beta_two * moment_two + (1.0 - beta_two) * gradient * gradient
    corrected_one = new_one / (1.0 - beta_one**STEP)
    corrected_two = new_two / (1.0 - beta_two**STEP)
    new_weight = weight - rate * (
        corrected_one / (jnp.sqrt(corrected_two) + adam_eps) + decay * weight
    )
    return (new_weight, new_one, new_two)


def exchange(block, axis, step):
    count = lax.axis_size(axis)
    return lax.ppermute(block, axis, [(i, i ^ step) for i in range(count)])


MESH_ID = pl.DeviceIdType.MESH


def rolled(vectors, sine_table):
    width = vectors.shape[1]
    half_width = HEAD_SIZE // 2
    lane = lax.broadcasted_iota(jnp.int32, vectors.shape, 1)
    ahead = pltpu.roll(vectors, width - half_width, 1)
    behind = pltpu.roll(vectors, half_width, 1)
    return jnp.where(lane % HEAD_SIZE < half_width, ahead, behind) * sine_table


def causal_mask(count):
    row = lax.broadcasted_iota(jnp.int32, (count, count), 0)
    column = lax.broadcasted_iota(jnp.int32, (count, count), 1)
    allowed = row >= column
    if count > SEQ:
        allowed = allowed & (row // SEQ == column // SEQ)
    return allowed


def dot_last(left, right):
    return lax.dot_general(
        left, right, (((1,), (1,)), ((), ())), preferred_element_type=jnp.float32
    )


def dot_first(left, right):
    return lax.dot_general(
        left, right, (((0,), (0,)), ((), ())), preferred_element_type=jnp.float32
    )


class Gather:
    def __init__(self, net, ref, sems, copies, relayed):
        self.net = net
        self.ref = ref
        self.sems = sems
        self.copies = copies
        self.relayed = relayed

    def wait(self, index):
        net = self.net
        self.copies[index].wait_recv()
        if self.relayed and index == 0:
            inner = (net.z == 1) | (net.z == 2)
            source = (net.z + 2) % 4
            target = net.z + 1 - 2 * (net.z % 2)
            copy = pltpu.make_async_remote_copy(
                src_ref=self.ref.at[source],
                dst_ref=self.ref.at[source],
                send_sem=self.sems.at[0, 0],
                recv_sem=self.sems.at[1, (target + 4 - source) % 4],
                device_id=(net.me, target),
                device_id_type=MESH_ID,
            )
            pl.when(inner)(copy.start)
            net.sent_if.append((inner, copy))

    def wait_all(self):
        for index in range(len(self.copies)):
            self.wait(index)


class Links:
    def __init__(self, dp_count, z_count):
        self.dp_count = dp_count
        self.z_count = z_count
        self.me = lax.axis_index("dp")
        self.z = lax.axis_index("tensor")
        self.sibling = self.me + 1 - 2 * (self.me % 2)
        self.sent = []
        self.sent_if = []

    def barrier(self):
        semaphore = pltpu.get_barrier_semaphore()
        peers = [((self.me + s) % self.dp_count, self.z) for s in range(1, self.dp_count)]
        peers += [(self.me, (self.z + s) % self.z_count) for s in range(1, self.z_count)]
        for peer in peers:
            pl.semaphore_signal(semaphore, inc=1, device_id=peer, device_id_type=MESH_ID)
        pl.semaphore_wait(semaphore, len(peers))

    def send(self, source, target, send_sem, recv_sem, device):
        copy = pltpu.make_async_remote_copy(
            src_ref=source,
            dst_ref=target,
            send_sem=send_sem,
            recv_sem=recv_sem,
            device_id=device,
            device_id_type=MESH_ID,
        )
        copy.start()
        self.sent.append(copy)
        return copy

    def dp_peers(self):
        return [(s, (self.me + s) % self.dp_count) for s in range(1, self.dp_count)]

    def z_peers(self):
        order = sorted(range(1, self.z_count), key=lambda s: abs(s - self.z_count // 2))
        return [(s, (self.z + s) % self.z_count) for s in order]

    def z_gather(self, ref, sems):
        relayed = self.z_count == 4
        last = self.z_count - 1
        copies = []
        for s, p in self.z_peers():
            copy = pltpu.make_async_remote_copy(
                src_ref=ref.at[self.z],
                dst_ref=ref.at[self.z],
                send_sem=sems.at[0, s],
                recv_sem=sems.at[1, s],
                device_id=(self.me, p),
                device_id_type=MESH_ID,
            )
            if relayed and s != 2:
                direct = self.z != (0 if s == last else last)
                pl.when(direct)(copy.start)
                self.sent_if.append((direct, copy))
            else:
                copy.start()
                self.sent.append(copy)
            copies.append(copy)
        return Gather(self, ref, sems, copies, relayed)

    def z_scatter(self, ref, land, sems):
        return [
            self.send(ref.at[p], land.at[self.z], sems.at[0, s], sems.at[1, s], (self.me, p))
            for s, p in self.z_peers()
        ]

    def z_sources(self):
        return [(self.z + self.z_count - s) % self.z_count for s, _ in self.z_peers()]

    def finish(self):
        for copy in self.sent:
            copy.wait_send()
        for started, copy in self.sent_if:
            pl.when(started)(copy.wait_send)


def forward_kernel(
    dp_count,
    z_count,
    block_in,
    cotangent,
    gains_wide,
    attn_rows,
    expert_rows,
    cos_table,
    sine_table,
    residual,
    tokens_pair,
    cot_pair,
    whole_rows,
    attn_all,
    gains_all,
    tokens_one,
    rotated,
    attended,
    log_totals,
    gains_land,
    part,
    land,
    gain_sems,
    attn_sems,
    expert_sems,
    one_sems,
    cot_sems,
    land_sems,
    two_sems,
    pair_sems,
    own_sem,
):
    bf = jnp.bfloat16
    f32 = jnp.float32
    net = Links(dp_count, z_count)
    me, z, sibling = net.me, net.z, net.sibling
    own_rows, width = block_in.shape
    tok_count = z_count * own_rows
    cols = attn_rows.shape[1] // 6
    net.barrier()
    gain_copies = [
        net.send(gains_wide, gains_land.at[me], gain_sems.at[0, s], gain_sems.at[1, s], (p, z))
        for s, p in net.dp_peers()
    ]
    attn_copies = [
        net.send(attn_rows, attn_all.at[me], attn_sems.at[0, s], attn_sems.at[1, s], (p, z))
        for s, p in net.dp_peers()
    ]
    cot_pair[0, z] = cotangent[...].astype(bf)
    attn_all[me] = attn_rows[...]
    gains_land[me] = gains_wide[...]
    block = block_in[...]
    inv_one = lax.rsqrt(jnp.mean(block * block, axis=1, keepdims=True) + norm_eps)
    for copy in gain_copies:
        copy.wait_recv()
    gains = gains_land[0]
    for i in range(1, dp_count):
        gains = gains + gains_land[i]
    gains_all[...] = gains
    tokens_one[z] = (block * inv_one * gains[0:1]).astype(bf)
    one_copies = net.z_gather(tokens_one, one_sems)
    expert_copies = [
        net.send(
            expert_rows.at[p % 2],
            whole_rows.at[me],
            expert_sems.at[0, s],
            expert_sems.at[1, s],
            (p, z),
        )
        for s, p in net.dp_peers()
    ]
    own_copy = pltpu.make_async_copy(expert_rows.at[me % 2], whole_rows.at[me], own_sem)
    own_copy.start()

    def to_sibling(ref, index, slot):
        return net.send(
            ref.at[0, index],
            ref.at[1, index],
            pair_sems.at[0, slot],
            pair_sems.at[1, slot],
            (sibling, z),
        )

    pair_copies = []
    one_copies.wait_all()
    for copy in attn_copies:
        copy.wait_recv()
    cot_copies = net.z_gather(cot_pair.at[0], cot_sems)
    pair_copies.append(to_sibling(cot_pair, z, 0))
    weights = attn_all[...].reshape(dp_count * attn_rows.shape[0], 6 * cols)
    tokens = tokens_one[...].reshape(tok_count, width)
    projected = jnp.dot(tokens, weights[:, : 4 * cols], preferred_element_type=f32)
    cosines = cos_table[...]
    sines = sine_table[...]
    for i in range(3):
        vectors = projected[:, i * cols : (i + 1) * cols]
        rotated[:, i * cols : (i + 1) * cols] = (
            vectors * cosines + rolled(vectors, sines)
        ).astype(bf)
    rotated[:, 3 * cols :] = projected[:, 3 * cols :].astype(bf)
    allowed = causal_mask(tok_count)
    scale = HEAD_SIZE ** (-0.5)
    totals = []
    for j in range(2):
        heads = []
        for g in range(cols // HEAD_SIZE):
            at = g * HEAD_SIZE
            query = rotated[:, j * cols + at : j * cols + at + HEAD_SIZE]
            key = rotated[:, 2 * cols + at : 2 * cols + at + HEAD_SIZE]
            value = rotated[:, 3 * cols + at : 3 * cols + at + HEAD_SIZE]
            scores = jnp.where(allowed, dot_last(query, key) * scale, -1e30)
            top = jnp.max(scores, axis=1, keepdims=True)
            total = top + jnp.log(jnp.sum(jnp.exp(scores - top), axis=1, keepdims=True))
            softmax = jnp.exp(scores - total).astype(bf)
            heads.append(jnp.dot(softmax, value, preferred_element_type=f32).astype(bf))
            totals.append(total)
        attended[:, j * cols : (j + 1) * cols] = jnp.concatenate(heads, axis=1)
    for i, total in enumerate(totals):
        log_totals[i] = total
    partial_value = dot_last(attended[...], weights[:, 4 * cols :])
    part[...] = partial_value.astype(bf).reshape(z_count, own_rows, width)
    land_copies = net.z_scatter(part, land, land_sems)
    for i, source in enumerate(net.z_sources()):
        cot_copies.wait(i)
        pair_copies.append(to_sibling(cot_pair, source, 1 + i))
    for copy in land_copies:
        copy.wait_recv()
    total = block + part[z].astype(f32)
    for source in net.z_sources():
        total = total + land[source].astype(f32)
    residual[...] = total
    inv_two = lax.rsqrt(jnp.mean(total * total, axis=1, keepdims=True) + norm_eps)
    tokens_pair[0, z] = (total * inv_two * gains[1:2]).astype(bf)
    two_copies = net.z_gather(tokens_pair.at[0], two_sems)
    pair_copies.append(to_sibling(tokens_pair, z, z_count))
    for i, source in enumerate(net.z_sources()):
        two_copies.wait(i)
        pair_copies.append(to_sibling(tokens_pair, source, z_count + 1 + i))
    for copy in pair_copies + expert_copies:
        copy.wait_recv()
    own_copy.wait()
    net.finish()


def backward_kernel(
    dp_count,
    z_count,
    back,
    mixture,
    grads,
    residual_in,
    cotangent,
    block_in,
    gains_all,
    tokens_one,
    rotated,
    attended,
    log_totals,
    attn_all,
    cos_table,
    sine_table,
    grads_land,
    attn_land,
    block_out,
    input_grad,
    back_land,
    mix_land,
    part,
    land,
    resid_all,
    norm_part,
    norm_land,
    mix_part,
    mix_sum_land,
    attn_local,
    grad_sems,
    attn_sems,
    pair_sems,
    land_sems,
    resid_sems,
    norm_sems,
    mix_sems,
    own_sem,
):
    bf = jnp.bfloat16
    f32 = jnp.float32
    net = Links(dp_count, z_count)
    me, z, sibling = net.me, net.z, net.sibling
    own_rows, width = block_in.shape
    tok_count = z_count * own_rows
    rows = attn_all.shape[1]
    cols = attn_all.shape[2] // 6
    net.barrier()
    back_copy = net.send(
        back.at[1], back_land, pair_sems.at[0, 0], pair_sems.at[1, 0], (sibling, z)
    )
    mix_copy = net.send(
        mixture.at[1], mix_land, pair_sems.at[0, 1], pair_sems.at[1, 1], (sibling, z)
    )
    grad_copies = [
        net.send(
            grads.at[p], grads_land.at[me], grad_sems.at[0, s], grad_sems.at[1, s], (p, z)
        )
        for s, p in net.dp_peers()
    ]
    own_copy = pltpu.make_async_copy(grads.at[me], grads_land.at[me], own_sem)
    own_copy.start()
    back_copy.wait_recv()
    part[...] = (back[0].astype(f32) + back_land[...].astype(f32)).astype(bf)
    land_copies = net.z_scatter(part, land, land_sems)
    mix_copy.wait_recv()
    mix_part[...] = (mixture[0].astype(f32) + mix_land[...].astype(f32)).astype(bf)
    residual = residual_in[...]
    gain_one = gains_all[0:1]
    gain_two = gains_all[1:2]
    inv_two = lax.rsqrt(jnp.mean(residual * residual, axis=1, keepdims=True) + norm_eps)
    for copy in land_copies:
        copy.wait_recv()
    normed_two_cot = part[z].astype(f32)
    for source in net.z_sources():
        normed_two_cot = normed_two_cot + land[source].astype(f32)
    scaled = gain_two * normed_two_cot
    residual_cot = (
        cotangent[...]
        + inv_two * scaled
        - residual
        * (inv_two * inv_two * inv_two * jnp.mean(scaled * residual, axis=1, keepdims=True))
    )
    input_grad[...] = residual_cot
    resid_all[z] = residual_cot.astype(bf)
    resid_copies = net.z_gather(resid_all, resid_sems)
    resid_copies.wait_all()
    mix_copies = net.z_scatter(mix_part, mix_sum_land, mix_sems)
    weights = attn_all[...].reshape(dp_count * rows, 6 * cols)
    resid = resid_all[...].reshape(tok_count, width)
    attended_cot = jnp.dot(resid, weights[:, 4 * cols :], preferred_element_type=f32).astype(bf)
    allowed = causal_mask(tok_count)
    scale = HEAD_SIZE ** (-0.5)
    heads = cols // HEAD_SIZE
    query_cots = [[None] * heads for _ in range(2)]
    key_cots = [None] * heads
    value_cots = [None] * heads
    for g in range(heads):
        at = g * HEAD_SIZE
        key = rotated[:, 2 * cols + at : 2 * cols + at + HEAD_SIZE]
        value = rotated[:, 3 * cols + at : 3 * cols + at + HEAD_SIZE]
        for j in range(2):
            query = rotated[:, j * cols + at : j * cols + at + HEAD_SIZE]
            cot = attended_cot[:, j * cols + at : j * cols + at + HEAD_SIZE]
            seen = attended[:, j * cols + at : j * cols + at + HEAD_SIZE]
            scores = jnp.where(allowed, dot_last(query, key) * scale, -1e30)
            softmax = jnp.exp(scores - log_totals[j * heads + g])
            dots = jnp.sum(cot.astype(f32) * seen.astype(f32), axis=1, keepdims=True)
            score_cot = (softmax * (dot_last(cot, value) - dots)).astype(bf)
            value_cot = dot_first(softmax.astype(bf), cot)
            key_cot = dot_first(score_cot, query) * scale
            query_cots[j][g] = jnp.dot(score_cot, key, preferred_element_type=f32) * scale
            value_cots[g] = value_cot if j == 0 else value_cots[g] + value_cot
            key_cots[g] = key_cot if j == 0 else key_cots[g] + key_cot
    cosines = cos_table[...]
    sines = sine_table[...]

    def unrotated(parts):
        vectors = jnp.concatenate(parts, axis=1)
        return (vectors * cosines - rolled(vectors, sines)).astype(bf)

    proj_cot = jnp.concatenate(
        [
            unrotated(query_cots[0]),
            unrotated(query_cots[1]),
            unrotated(key_cots),
            jnp.concatenate(value_cots, axis=1).astype(bf),
        ],
        axis=1,
    )
    norm_terms = dot_last(proj_cot, weights[:, : 4 * cols])
    norm_part[...] = norm_terms.astype(bf).reshape(z_count, own_rows, width)
    norm_copies = net.z_scatter(norm_part, norm_land, norm_sems)
    tokens = tokens_one[...].reshape(tok_count, width)
    attn_local[:, :, : 4 * cols] = (
        dot_first(tokens, proj_cot).astype(bf).reshape(dp_count, rows, 4 * cols)
    )
    attn_local[:, :, 4 * cols :] = (
        dot_first(resid, attended[...]).astype(bf).reshape(dp_count, rows, 2 * cols)
    )
    attn_copies = [
        net.send(
            attn_local.at[p], attn_land.at[me], attn_sems.at[0, s], attn_sems.at[1, s], (p, z)
        )
        for s, p in net.dp_peers()
    ]
    attn_land[me] = attn_local[me]
    for copy in mix_copies:
        copy.wait_recv()
    total = residual + mix_part[z].astype(f32)
    for source in net.z_sources():
        total = total + mix_sum_land[source].astype(f32)
    block_out[...] = total
    block = block_in[...]
    inv_one = lax.rsqrt(jnp.mean(block * block, axis=1, keepdims=True) + norm_eps)
    for copy in norm_copies:
        copy.wait_recv()
    normed_one_cot = norm_part[z].astype(f32)
    for source in net.z_sources():
        normed_one_cot = normed_one_cot + norm_land[source].astype(f32)
    scaled = gain_one * normed_one_cot
    input_grad[...] = (
        input_grad[...]
        + inv_one * scaled
        - block * (inv_one * inv_one * inv_one * jnp.mean(scaled * block, axis=1, keepdims=True))
    )
    for copy in attn_copies + grad_copies:
        copy.wait_recv()
    own_copy.wait()
    net.finish()


def in_vmem(count):
    return [pl.BlockSpec(memory_space=pltpu.VMEM)] * count


def in_place(count):
    return [pl.BlockSpec(memory_space=pl.ANY)] * count


def local(
    block_in,
    cotangent,
    routes,
    gate_weights,
    norm_gains,
    attention_weight,
    output_weight,
    w_gate_up,
    w_down,
    m_gains,
    v_gains,
    attention_first_moment,
    attention_second_moment,
    output_first_moment,
    output_second_moment,
    m_gate_up,
    v_gate_up,
    m_down,
    v_down,
):
    bf = jnp.bfloat16
    f32 = jnp.float32
    tok_count = routes.shape[0]
    own_rows, width = block_in.shape
    experts = w_gate_up.shape[0]
    rows = w_gate_up.shape[2]
    units = w_gate_up.shape[3]
    cols = attention_weight.shape[2]
    dp_count = lax.axis_size("dp")
    z_count = lax.axis_size("tensor")
    me = lax.axis_index("dp")
    parity = me % 2
    held = experts // 2
    half = held * units
    shape = jax.ShapeDtypeStruct
    dma = pltpu.SemaphoreType.DMA
    block_of = (z_count, own_rows, width)

    attn_rows = jnp.concatenate([attention_weight, output_weight], axis=0)
    attn_rows = attn_rows.astype(bf).transpose(1, 0, 2).reshape(rows, 6 * cols)
    gate_up_b = w_gate_up.astype(bf)
    down_b = w_down.astype(bf)
    expert_rows = jnp.concatenate([gate_up_b, down_b[:, None]], axis=1)
    expert_rows = (
        expert_rows.reshape(2, held, 3, rows, units)
        .transpose(0, 3, 2, 1, 4)
        .reshape(2, rows, 3 * half)
    )
    gains_wide = lax.dynamic_update_slice_in_dim(
        jnp.zeros((2, width), f32), norm_gains.astype(bf).astype(f32), me * rows, axis=1
    )
    cos_table, sine_table = rope_tables(tok_count, cols)

    (
        residual,
        tokens_pair,
        cot_pair,
        whole_rows,
        attn_all,
        gains_all,
        tokens_one,
        rotated,
        attended,
        log_totals,
    ) = pl.pallas_call(
        functools.partial(forward_kernel, dp_count, z_count),
        out_shape=(
            shape((own_rows, width), f32),
            shape((2,) + block_of, bf),
            shape((2,) + block_of, bf),
            shape((dp_count, rows, 3 * half), bf),
            shape((dp_count, rows, 6 * cols), bf),
            shape((2, width), f32),
            shape(block_of, bf),
            shape((tok_count, 4 * cols), bf),
            shape((tok_count, 2 * cols), bf),
            shape((2 * cols // HEAD_SIZE, tok_count, 1), f32),
        ),
        in_specs=in_vmem(4) + in_place(1) + in_vmem(2),
        out_specs=in_vmem(3) + in_place(1) + in_vmem(6),
        scratch_shapes=[
            pltpu.VMEM((dp_count, 2, width), f32),
            pltpu.VMEM(block_of, bf),
            pltpu.VMEM(block_of, bf),
            dma((2, dp_count)),
            dma((2, dp_count)),
            dma((2, dp_count)),
            dma((2, z_count)),
            dma((2, z_count)),
            dma((2, z_count)),
            dma((2, z_count)),
            dma((2, 2 * z_count)),
            dma,
        ],
        compiler_params=pltpu.CompilerParams(
            collective_id=0, has_side_effects=True, vmem_limit_bytes=48 * 1024 * 1024
        ),
        name="forward_kernel",
    )(block_in, cotangent, gains_wide, attn_rows, expert_rows, cos_table, sine_table)

    expert_ids = jnp.arange(experts, dtype=jnp.int32)[None, None, :]
    token_weight = jnp.sum(
        jnp.where(routes[:, :, None] == expert_ids, gate_weights[:, :, None], 0.0), axis=1
    )
    token_weight = token_weight.reshape(tok_count, 2, held)
    weight_mine = lax.dynamic_index_in_dim(token_weight, parity, 1, False)
    weight_other = lax.dynamic_index_in_dim(token_weight, 1 - parity, 1, False)
    weight_pair = jnp.concatenate([weight_mine, exchange(weight_other, "dp", 1)], axis=0)
    weight_wide = jnp.broadcast_to(
        weight_pair[:, :, None], (2 * tok_count, held, units)
    ).reshape(2 * tok_count, half)

    tokens_pair = tokens_pair.reshape(2 * tok_count, width)
    cot_pair = cot_pair.reshape(2 * tok_count, width)
    whole_rows = whole_rows.reshape(dp_count * rows, 3 * half)
    gate_up_all = whole_rows[:, : 2 * half]
    down_all = whole_rows[:, 2 * half :]
    gate_up = jnp.dot(tokens_pair, gate_up_all, preferred_element_type=f32)
    gate_vals = gate_up[:, :half]
    up_vals = gate_up[:, half:]
    sigmoid_vals = jax.nn.sigmoid(gate_vals)
    hidden = (gate_vals * sigmoid_vals * up_vals * weight_wide).astype(bf)
    hidden_cot = jnp.dot(cot_pair, down_all, preferred_element_type=f32) * weight_wide
    gate_cot = (
        hidden_cot * up_vals * sigmoid_vals * (1.0 + gate_vals * (1.0 - sigmoid_vals))
    ).astype(bf)
    up_cot = (hidden_cot * gate_vals * sigmoid_vals).astype(bf)
    both_cot = jnp.concatenate([gate_cot, up_cot], axis=1)
    back = dot_last(both_cot, gate_up_all).astype(bf)
    mixture = dot_last(hidden, down_all).astype(bf)
    gate_up_local = dot_first(tokens_pair, both_cot).astype(bf)
    down_local = dot_first(cot_pair, hidden).astype(bf)
    grads_local = jnp.concatenate([gate_up_local, down_local], axis=1)
    grads_local = grads_local.reshape(dp_count, rows, 3 * held, units).transpose(0, 2, 1, 3)

    grads_land, attn_land, block_out, input_grad = pl.pallas_call(
        functools.partial(backward_kernel, dp_count, z_count),
        out_shape=(
            shape((dp_count, 3 * held, rows, units), bf),
            shape((dp_count, rows, 6 * cols), bf),
            shape((own_rows, width), f32),
            shape((own_rows, width), f32),
        ),
        in_specs=in_vmem(2) + in_place(1) + in_vmem(11),
        out_specs=in_place(1) + in_vmem(3),
        scratch_shapes=[
            pltpu.VMEM(block_of, bf),
            pltpu.VMEM(block_of, bf),
            pltpu.VMEM(block_of, bf),
            pltpu.VMEM(block_of, bf),
            pltpu.VMEM(block_of, bf),
            pltpu.VMEM(block_of, bf),
            pltpu.VMEM(block_of, bf),
            pltpu.VMEM(block_of, bf),
            pltpu.VMEM(block_of, bf),
            pltpu.VMEM((dp_count, rows, 6 * cols), bf),
            dma((2, dp_count)),
            dma((2, dp_count)),
            dma((2, 2)),
            dma((2, z_count)),
            dma((2, z_count)),
            dma((2, z_count)),
            dma((2, z_count)),
            dma,
        ],
        compiler_params=pltpu.CompilerParams(
            collective_id=1, has_side_effects=True, vmem_limit_bytes=56 * 1024 * 1024
        ),
        name="backward_kernel",
    )(
        back.reshape((2,) + block_of),
        mixture.reshape((2,) + block_of),
        grads_local,
        residual,
        cotangent,
        block_in,
        gains_all,
        tokens_one,
        rotated,
        attended,
        log_totals,
        attn_all,
        cos_table,
        sine_table,
    )

    both_sum = jnp.sum(attn_land.astype(f32), axis=0)
    both_sum = both_sum.reshape(rows, 6, cols).transpose(1, 0, 2)
    grad_attn = both_sum[:4]
    grad_out = both_sum[4:]
    grads_land = grads_land.reshape(dp_count // 2, 2, 3, held, rows, units)
    expert_sum = grads_land[0].astype(f32)
    for i in range(1, dp_count // 2):
        expert_sum = expert_sum + grads_land[i].astype(f32)
    expert_sum = expert_sum.transpose(0, 2, 1, 3, 4).reshape(experts, 3, rows, units)
    grad_gate_up = expert_sum[:, :2]
    grad_down = expert_sum[:, 2]
    gain_local = jnp.stack(
        [
            jnp.sum(attention_weight.astype(bf).astype(f32) * grad_attn, axis=(0, 2)),
            jnp.sum(gate_up_b.astype(f32) * grad_gate_up, axis=(0, 1, 3)),
        ]
    )
    gain_sum = gain_local
    for step in range(1, z_count):
        gain_sum = gain_sum + exchange(gain_local, "tensor", step)
    grad_gains = gain_sum / norm_gains.astype(bf).astype(f32)
    new_gains, new_m_gains, new_v_gains = adamw_update(
        norm_gains, m_gains, v_gains, grad_gains, rate_gain, 0.0
    )
    new_attn, new_m_attn, new_v_attn = adamw_update(
        attention_weight,
        attention_first_moment,
        attention_second_moment,
        grad_attn,
        rate_matrix,
        decay_matrix,
    )
    new_out, new_m_out, new_v_out = adamw_update(
        output_weight,
        output_first_moment,
        output_second_moment,
        grad_out,
        rate_matrix,
        decay_matrix,
    )
    new_gate_up, new_m_gate_up, new_v_gate_up = adamw_update(
        w_gate_up, m_gate_up, v_gate_up, grad_gate_up, rate_matrix, decay_matrix
    )
    new_down, new_m_down, new_v_down = adamw_update(
        w_down, m_down, v_down, grad_down, rate_matrix, decay_matrix
    )
    return (
        block_out,
        input_grad,
        grad_gains,
        grad_attn,
        grad_out,
        grad_gate_up,
        grad_down,
        new_gains,
        new_attn,
        new_out,
        new_gate_up,
        new_down,
        new_m_gains,
        new_v_gains,
        new_m_attn,
        new_v_attn,
        new_m_out,
        new_v_out,
        new_m_gate_up,
        new_v_gate_up,
        new_m_down,
        new_v_down,
    )


def solution(mesh):
    return jax.shard_map(
        local,
        mesh=mesh,
        in_specs=(
            P(("dp", "tensor"), None),
            P(("dp", "tensor"), None),
            P("dp", None),
            P("dp", None),
            P(None, "dp"),
            P(None, "dp", "tensor"),
            P(None, "dp", "tensor"),
            P(None, None, "dp", "tensor"),
            P(None, "dp", "tensor"),
            P(None, "dp"),
            P(None, "dp"),
            P(None, "dp", "tensor"),
            P(None, "dp", "tensor"),
            P(None, "dp", "tensor"),
            P(None, "dp", "tensor"),
            P(None, None, "dp", "tensor"),
            P(None, None, "dp", "tensor"),
            P(None, "dp", "tensor"),
            P(None, "dp", "tensor"),
        ),
        out_specs=(
            P(("dp", "tensor"), None),
            P(("dp", "tensor"), None),
            P(None, "dp"),
            P(None, "dp", "tensor"),
            P(None, "dp", "tensor"),
            P(None, None, "dp", "tensor"),
            P(None, "dp", "tensor"),
            P(None, "dp"),
            P(None, "dp", "tensor"),
            P(None, "dp", "tensor"),
            P(None, None, "dp", "tensor"),
            P(None, "dp", "tensor"),
            P(None, "dp"),
            P(None, "dp"),
            P(None, "dp", "tensor"),
            P(None, "dp", "tensor"),
            P(None, "dp", "tensor"),
            P(None, "dp", "tensor"),
            P(None, None, "dp", "tensor"),
            P(None, None, "dp", "tensor"),
            P(None, "dp", "tensor"),
            P(None, "dp", "tensor"),
        ),
        check_vma=False,
    )
```
